32 devices in a mesh: weight: 4 (over y, x), context: 2 (over core), tensor: 4 (over z).
Axes of the slice: x: 2, y: 2, z: 4, core: 2. Of those that a mesh axis runs over, the one named last changes fastest.
Arguments:
- block_input: bfloat16 [4, 1024, 1024], P('weight', ('context', 'tensor')), may hold values from -6 to 6
- block_ids: int32 [4, 1024], P('weight'), may hold values from 0 to 7, never falling along the last dimension, each value on 1 to 256 neighbouring positions
- adapter_index: int32 [4], P('weight'), may hold values from 0 to 3, each once
- ln1_gain: bfloat16 [1024], replicated, may hold values from 0.5 to 1.5
- ln1_bias: bfloat16 [1024], replicated, may hold values from -1.796875 to 1.796875
- w_qkv: bfloat16 [1024, 3, 1024], P('weight', None, 'tensor'), may hold values from -0.1875 to 0.1875
- qv_bias: bfloat16 [2, 1024], P(None, 'tensor'), may hold values from -1.1953125 to 1.1953125
- w_out: bfloat16 [1024, 1024], P('tensor', 'weight'), may hold values from -0.75 to 0.75
- out_bias: bfloat16 [1024], replicated, may hold values from -1.796875 to 1.796875
- ln2_gain: bfloat16 [1024], replicated, may hold values from 0.5 to 1.5
- ln2_bias: bfloat16 [1024], replicated, may hold values from -1.796875 to 1.796875
- w_up: bfloat16 [1024, 4096], P('weight', 'tensor'), may hold values from -0.1875 to 0.1875
- up_bias: bfloat16 [4096], P('tensor'), may hold values from -1.796875 to 1.796875
- w_down: bfloat16 [4096, 1024], P('tensor', 'weight'), may hold values from -0.09375 to 0.09375
- down_bias: bfloat16 [1024], replicated, may hold values from -1.796875 to 1.796875
- qkv_a: bfloat16 [4, 1024, 16], replicated, may hold values from -0.1875 to 0.1875
- qkv_b: bfloat16 [4, 16, 3, 1024], P(None, None, None, 'tensor'), may hold values from -0.75 to 0.75
- out_a: bfloat16 [4, 1024, 16], P(None, 'tensor'), may hold values from -0.75 to 0.75
- out_b: bfloat16 [4, 16, 1024], replicated, may hold values from -0.75 to 0.75
- up_a: bfloat16 [4, 1024, 16], replicated, may hold values from -0.1875 to 0.1875
- up_b: bfloat16 [4, 16, 4096], P(None, None, 'tensor'), may hold values from -0.75 to 0.75
- down_a: bfloat16 [4, 4096, 16], P(None, 'tensor'), may hold values from -0.09375 to 0.09375
- down_b: bfloat16 [4, 16, 1024], replicated, may hold values from -0.75 to 0.75
- cotangent: bfloat16 [4, 1024, 1024], P('weight', ('context', 'tensor')), may hold values from -6 to 6
Outputs:
- block_out: bfloat16 [4, 1024, 1024], P('weight', ('context', 'tensor'))
- x_grad: bfloat16 [4, 1024, 1024], P('weight', ('context', 'tensor'))
- qkv_a_grad: float32 [4, 1024, 16], replicated
- qkv_b_grad: float32 [4, 16, 3, 1024], P(None, None, None, 'tensor')
- out_a_grad: float32 [4, 1024, 16], P(None, 'tensor')
- out_b_grad: float32 [4, 16, 1024], replicated
- up_a_grad: float32 [4, 1024, 16], replicated
- up_b_grad: float32 [4, 16, 4096], P(None, None, 'tensor')
- down_a_grad: float32 [4, 4096, 16], P(None, 'tensor')
- down_b_grad: float32 [4, 16, 1024], replicated
The draws below stay inside these ranges and needn't reach their ends.
Inputs may be any that keep to these rules, and one draw needn't show every extreme that they name: `block_ids`: along each sequence the ids never fall; each block has 1 to 256 tokens, some block exactly 256; every id is used. `adapter_index`: each adapter belongs to exactly one sequence.
All inputs are finite; a program needn't handle non-finite values.
Results may differ from the reference program's by a relative error of at most 0.024.
Values may be sent and summed in bfloat16 or wider, within the bound.
No kernel may reach another device: no remote copies, remote signals or barrier semaphores. Data moves between devices by JAX's collectives and lax.ppermute only.
A program may use at most 192 MiB of HBM per device.

```python
import math
import jax
import jax.numpy as jnp
import numpy as np
from jax import lax

D = 1024
HEADS = 16
HEAD = 64
FF = 4096
RANK = 16
BLOCK = 256
SEQS = 4
ADAPTERS = 4
LENGTH = 1024
BLOCKS = 8


def shard_levels(own_key, shape, cuts, low, top_value):
    def one(position, shards_of):
        steps = jax.random.uniform(jax.random.fold_in(jax.random.fold_in(own_key, 6), position), (shards_of,), jnp.float32, low / len(cuts), top_value / len(cuts))
        return jnp.repeat(jnp.exp(steps), shape[position] // shards_of).reshape((-1,) + (1,) * (len(shape) - position - 1))

    loudness = one(*cuts[0])
    for cut in cuts[1:]:
        loudness = loudness * one(*cut)
    return loudness


def split_up(count, total, most, skew):
    portions = [(1 << 20) // math.isqrt(rank ** skew) + 1 for rank in range(2, count + 1)]
    rest, holding = total - most - (count - 1), [1] * (count - 1)
    while rest > 0:
        free = [i for i in range(count - 1) if holding[i] < most]
        mass, budget = sum([portions[i] for i in free]), rest
        for i in free:
            extra = min(most - holding[i], max(1, budget * portions[i] // mass), rest)
            holding[i] = holding[i] + extra
            rest = rest - extra
    return np.array([most] + holding)


def ragged_sizes(stream_key, amount, total, limit, slope):
    if amount == 2:
        one = jax.random.randint(stream_key, (), max(1, total - limit), min(limit, total - 1) + 1)
        return jnp.stack([one, total - one])
    sizes = jnp.asarray(split_up(amount, total, limit, slope), jnp.int32)
    couples = (amount - 1) // 2
    donor, sink = sizes[1:1 + 2 * couples:2], sizes[2:2 + 2 * couples:2]
    margin = jnp.minimum(donor - 1, limit - sink)
    passed = jax.random.randint(jax.random.fold_in(stream_key, 1), (couples,), 0, 1 << 20) % (margin + 1)
    sizes = sizes.at[1:1 + 2 * couples:2].set(donor - passed).at[2:2 + 2 * couples:2].set(sink + passed)
    return sizes[jax.random.permutation(jax.random.fold_in(stream_key, 2), amount)]


def scatter_about(own_key, dims, scale, bound, cuts=(), dtype=jnp.bfloat16):
    loudness = shard_levels(own_key, dims, cuts, -0.22, 0.18) if cuts else 1.0
    values = jax.random.normal(own_key, dims, jnp.float32) * scale * loudness
    return jnp.minimum(jnp.maximum(values, -bound), bound).astype(dtype)


def setup_inputs(seed: int = 0) -> dict:
    key_of = jax.random.split(jax.random.key(seed), 25)
    return {
        "block_input": scatter_about(key_of[0], (SEQS, LENGTH, D), 1.0, 6.0, ((0, 4), (1, 8))),
        "block_ids": jax.vmap(lambda own: jnp.searchsorted(jnp.cumsum(ragged_sizes(own, BLOCKS, LENGTH, BLOCK, 0)), jnp.arange(LENGTH), side="right"))(jax.random.split(key_of[1], SEQS)).reshape((SEQS, LENGTH)).astype(jnp.int32),
        "adapter_index": jax.random.permutation(key_of[2], ADAPTERS).astype(jnp.int32),
        "ln1_gain": jnp.clip(1.0 + 0.1 * jax.random.normal(key_of[3], (D,), jnp.float32), 0.5, 1.5).astype(jnp.bfloat16),
        "ln1_bias": scatter_about(key_of[4], (D,), 0.3, 1.796875),
        "w_qkv": scatter_about(key_of[5], (D, 3, D), D ** -0.5, 0.1875, ((0, 4), (2, 4))),
        "qv_bias": scatter_about(key_of[6], (2, D), 0.2, 1.1953125, ((1, 4),)),
        "w_out": scatter_about(key_of[7], (D, D), (D // 16) ** -0.5, 0.75, ((0, 4), (1, 4))),
        "out_bias": scatter_about(key_of[8], (D,), 0.3, 1.796875),
        "ln2_gain": jnp.clip(1.0 + 0.1 * jax.random.normal(key_of[9], (D,), jnp.float32), 0.5, 1.5).astype(jnp.bfloat16),
        "ln2_bias": scatter_about(key_of[10], (D,), 0.3, 1.796875),
        "w_up": scatter_about(key_of[11], (D, FF), D ** -0.5, 0.1875, ((0, 4), (1, 4))),
        "up_bias": scatter_about(key_of[12], (FF,), 0.3, 1.796875, ((0, 4),)),
        "w_down": scatter_about(key_of[13], (FF, D), FF ** -0.5, 0.09375, ((0, 4), (1, 4))),
        "down_bias": scatter_about(key_of[14], (D,), 0.3, 1.796875),
        "qkv_a": scatter_about(key_of[15], (ADAPTERS, D, RANK), D ** -0.5, 0.1875),
        "qkv_b": scatter_about(key_of[16], (ADAPTERS, RANK, 3, D), (4 * RANK) ** -0.5, 0.75, ((3, 4),)),
        "out_a": scatter_about(key_of[17], (ADAPTERS, D, RANK), (D // 16) ** -0.5, 0.75, ((1, 4),)),
        "out_b": scatter_about(key_of[18], (ADAPTERS, RANK, D), (4 * RANK) ** -0.5, 0.75),
        "up_a": scatter_about(key_of[19], (ADAPTERS, D, RANK), D ** -0.5, 0.1875),
        "up_b": scatter_about(key_of[20], (ADAPTERS, RANK, FF), (4 * RANK) ** -0.5, 0.75, ((2, 4),)),
        "down_a": scatter_about(key_of[21], (ADAPTERS, FF, RANK), FF ** -0.5, 0.09375, ((1, 4),)),
        "down_b": scatter_about(key_of[22], (ADAPTERS, RANK, D), (4 * RANK) ** -0.5, 0.75),
        "cotangent": scatter_about(key_of[23], (SEQS, LENGTH, D), 1.0, 6.0, ((0, 4), (1, 8))),
    }


HIGHEST = lax.Precision.HIGHEST

@jax.custom_vjp
def low(v):
    return lax.optimization_barrier(v.astype(jnp.bfloat16)).astype(jnp.float32)

@jax.custom_vjp
def low_back(v):
    return v

def low_keep(v):
    return (low(v), None)

def low_pass(kept, grad):
    return (grad,)

def back_keep(v):
    return (v, None)

def back_low(kept, grad):
    return (low(grad),)
low.defvjp(low_keep, low_pass)
low_back.defvjp(back_keep, back_low)

def matmul(left, right):
    return jnp.dot(left, right, preferred_element_type=jnp.float32, precision=HIGHEST)

def norm_rows(values, gain_vec, shift_vec):
    center = values - lax.optimization_barrier(jnp.mean(values, axis=-1, keepdims=True))
    spread = lax.optimization_barrier(jnp.mean(center * center, axis=-1, keepdims=True))
    return center * lax.rsqrt(spread + 1e-05) * gain_vec + shift_vec

def attend(queries, key_rows, value_rows, seq_ids):
    block_rows = min(512, LENGTH)
    block_count = LENGTH // block_rows
    score_scale = HEAD ** (-0.5)

    def one_block(inputs):
        block_q, block_ids_q = inputs
        scores = jnp.einsum('qhe,khe->hqk', block_q, key_rows, precision=HIGHEST) * score_scale
        scores = low_back(scores)
        allowed = seq_ids[None, None, :] <= block_ids_q[None, :, None]
        scores = jnp.where(allowed, scores, -1e+30)
        norm_log = jax.nn.logsumexp(scores, axis=-1, keepdims=True)
        prob_rows = low(jnp.exp(scores - norm_log))
        return jnp.einsum('hqk,khe->qhe', prob_rows, value_rows, precision=HIGHEST)
    pieces = lax.map(jax.checkpoint(one_block), (queries.reshape(block_count, block_rows, HEADS, HEAD), seq_ids.reshape(block_count, block_rows)))
    return pieces.reshape(LENGTH, HEADS * HEAD)

def forward(x_rows, seq_ids, adapter, tables, frozen):
    ln1_gain, ln1_bias, w_qkv, qv_bias, w_out, out_bias, ln2_gain, ln2_bias, w_up, up_bias, w_down, down_bias = frozen
    chosen = [lax.dynamic_index_in_dim(source, adapter, 0, keepdims=False) for source in tables]
    one_qkv_a, one_qkv_b, one_out_a, one_out_b, one_up_a, one_up_b, one_down_a, one_down_b = chosen
    normed_one = low(norm_rows(x_rows, ln1_gain, ln1_bias))
    low_qkv = low(low_back(matmul(normed_one, one_qkv_a)))
    projected = jnp.einsum('td,dcf->tcf', normed_one, w_qkv, precision=HIGHEST) + jnp.einsum('tr,rcf->tcf', low_qkv, one_qkv_b, precision=HIGHEST)
    bias_rows = jnp.stack([qv_bias[0], jnp.zeros_like(qv_bias[0]), qv_bias[1]])
    projected = low(low_back(projected + bias_rows))
    head_shape = (LENGTH, HEADS, HEAD)
    attended = attend(projected[:, 0].reshape(head_shape), projected[:, 1].reshape(head_shape), projected[:, 2].reshape(head_shape), seq_ids)
    attended = low(low_back(attended))
    low_out = low(low_back(matmul(attended, one_out_a)))
    middle = x_rows + low_back(matmul(attended, w_out) + matmul(low_out, one_out_b)) + out_bias
    normed_two = low(norm_rows(middle, ln2_gain, ln2_bias))
    low_up = low(low_back(matmul(normed_two, one_up_a)))
    up_pre = low_back(matmul(normed_two, w_up) + matmul(low_up, one_up_b) + up_bias)
    activated = low(jax.nn.gelu(up_pre, approximate=True))
    low_down = low(low_back(matmul(activated, one_down_a)))
    return middle + low_back(matmul(activated, w_down) + matmul(low_down, one_down_b)) + down_bias

def reference(block_input, block_ids, adapter_index, ln1_gain, ln1_bias, w_qkv, qv_bias, w_out, out_bias, ln2_gain, ln2_bias, w_up, up_bias, w_down, down_bias, qkv_a, qkv_b, out_a, out_b, up_a, up_b, down_a, down_b, cotangent):
    frozen = tuple((source.astype(jnp.float32) for source in (ln1_gain, ln1_bias, w_qkv, qv_bias, w_out, out_bias, ln2_gain, ln2_bias, w_up, up_bias, w_down, down_bias)))
    tables = tuple((source.astype(jnp.float32) for source in (qkv_a, qkv_b, out_a, out_b, up_a, up_b, down_a, down_b)))

    def one_sequence(totals, inputs):
        x_rows, seq_ids, adapter, seq_grad = inputs

        def apply_block(x_in, *table_in):
            return forward(x_in, seq_ids, adapter, table_in, frozen)
        result, pull_back = jax.vjp(apply_block, x_rows.astype(jnp.float32), *tables)
        gradients = pull_back(seq_grad.astype(jnp.float32))
        totals = tuple((running + gradient for running, gradient in zip(totals, gradients[1:])))
        return (totals, (result.astype(jnp.bfloat16), gradients[0].astype(jnp.bfloat16)))
    start_totals = tuple((jnp.zeros(source.shape, jnp.float32) for source in tables))
    totals, (block_out, x_grad) = lax.scan(one_sequence, start_totals, (block_input, block_ids, adapter_index, cotangent))
    return (block_out, x_grad, totals[0], totals[1], totals[2], totals[3], totals[4], totals[5], totals[6], totals[7])
```

```python
import jax
import jax.numpy as jnp
from jax import lax
from jax.experimental import pallas as pl
from jax.experimental.pallas import tpu as pltpu
from jax.sharding import PartitionSpec as P

HEAD = 64
BF = jnp.bfloat16
F32 = jnp.float32


def mm(left, right):
    return jnp.dot(left, right, preferred_element_type=F32)


def mm_nt(left, right):
    return lax.dot_general(left, right, (((1,), (1,)), ((), ())), preferred_element_type=F32)


def mm_tn(left, right):
    return lax.dot_general(left, right, (((0,), (0,)), ((), ())), preferred_element_type=F32)


def norm_stats(values):
    center = values - jnp.mean(values, axis=-1, keepdims=True)
    spread = jnp.mean(center * center, axis=-1, keepdims=True)
    scale = lax.rsqrt(spread + 1e-05)
    return center * scale, scale


def norm_back(unit, scale, grad):
    return (
        grad
        - jnp.mean(grad, axis=-1, keepdims=True)
        - unit * jnp.mean(grad * unit, axis=-1, keepdims=True)
    ) * scale


def gelu_tanh(values):
    return jax.nn.gelu(values, approximate=True)


def masked_scores(query_heads, key_rows, key_ids, query_ids):
    scores = jnp.einsum(
        "qhe,khe->hqk", query_heads, key_rows, preferred_element_type=F32
    ) * HEAD ** (-0.5)
    allowed = key_ids[None, None, :] <= query_ids[None, :, None]
    return jnp.where(allowed, scores, -1e30)


def fold_kernel(spot_ref, *refs):
    *part_refs, left_ref, right_ref, out_ref = refs
    step = pl.program_id(0)
    low = jnp.dot(
        left_ref[...].reshape(-1, left_ref.shape[-1]),
        right_ref[...],
        preferred_element_type=F32,
    ).reshape(out_ref.shape)
    for index, part_ref in enumerate(part_refs):

        @pl.when(step == index)
        def _():
            out_ref[...] = (part_ref[...].astype(F32) + low).astype(BF)


def fold(spots, parts, left, right, out_shape, part_block, left_spec, right_spec, out_spec):
    whole = [
        pl.BlockSpec(part_block, lambda i, s, n=len(part_block): (0,) * n) for _ in parts
    ]
    return pl.pallas_call(
        fold_kernel,
        out_shape=jax.ShapeDtypeStruct(out_shape, BF),
        grid_spec=pltpu.PrefetchScalarGridSpec(
            num_scalar_prefetch=1,
            grid=(len(parts),),
            in_specs=whole + [left_spec, right_spec],
            out_specs=out_spec,
        ),
    )(spots, *parts, left, right)


def make_device(n_weight, n_context, n_tensor):
    assert n_weight == 4 and n_tensor == 4 and n_context % 2 == 0

    def over(axis, size):
        def swap(value, bit):
            return lax.ppermute(value, axis, [(i, i ^ bit) for i in range(size)])

        return swap

    zx = over("tensor", n_tensor)
    wx = over("weight", n_weight)
    cx = over("context", n_context)

    def cross_edge(context, tensor):
        if (tensor % 2) + 2 * (context % 2) == tensor:
            return context, tensor
        return context ^ 1, tensor ^ 2

    cross_pairs = []
    for context in range(n_context):
        for tensor in range(n_tensor):
            to_context, to_tensor = cross_edge(context, tensor)
            cross_pairs.append((context * n_tensor + tensor, to_context * n_tensor + to_tensor))

    def cross(value):
        return lax.ppermute(value, ("context", "tensor"), cross_pairs)

    def context_sum(value):
        if n_context == 2:
            return value + cx(value.astype(BF), 1).astype(F32)
        return lax.psum(value, "context")

    def on_device(
        block_input,
        block_ids,
        adapter_index,
        ln1_gain,
        ln1_bias,
        w_qkv,
        qv_bias,
        w_out,
        out_bias,
        ln2_gain,
        ln2_bias,
        w_up,
        up_bias,
        w_down,
        down_bias,
        qkv_a,
        qkv_b,
        out_a,
        out_b,
        up_a,
        up_b,
        down_a,
        down_b,
        cotangent,
    ):
        wi = lax.axis_index("weight")
        ci = lax.axis_index("context")
        zi = lax.axis_index("tensor")
        parity = ci % 2
        home = (zi % 2) + 2 * parity == zi
        adapter = adapter_index[0]
        chosen = [
            lax.dynamic_index_in_dim(source, adapter, 0, keepdims=False)
            for source in (qkv_a, qkv_b, out_a, out_b, up_a, up_b, down_a, down_b)
        ]
        qa, qb, oa, ob, ua, ub, da, db = chosen
        width = qkv_a.shape[1]
        rank = qkv_a.shape[2]
        cols = qv_bias.shape[1]
        heads = cols // HEAD
        qb = qb.reshape(rank, 3 * cols)
        rows = block_input.shape[1]
        stretch = rows * n_tensor

        x = block_input[0].astype(F32)
        gain1 = ln1_gain.astype(F32)
        gain2 = ln2_gain.astype(F32)
        unit1, scale1 = norm_stats(x)
        h1 = (unit1 * gain1 + ln1_bias.astype(F32)).astype(BF)
        h1_1 = zx(h1, 1)
        h1_2 = zx(h1, 2)
        h1_3 = zx(h1_2, 1)
        h1s = jnp.concatenate([h1, h1_1, h1_2, h1_3], 0)

        half = w_qkv.shape[0] // 2
        wq_half = lax.dynamic_slice_in_dim(w_qkv, parity * half, half, 0).reshape(half, 3 * cols)
        spots = jnp.stack([wi ^ j for j in range(4)]).astype(jnp.int32)
        wq_parts = [wq_half] + [wx(wq_half, j) for j in (1, 2, 3)]
        wq_parts = wq_parts + [cx(part, 1) for part in wq_parts]
        wq = fold(
            jnp.concatenate([spots * 2 + parity, spots * 2 + 1 - parity]),
            wq_parts,
            qa,
            qb,
            (width, 3 * cols),
            (half, 3 * cols),
            pl.BlockSpec((half, rank), lambda i, s: (s[i], 0)),
            pl.BlockSpec((rank, 3 * cols), lambda i, s: (0, 0)),
            pl.BlockSpec((half, 3 * cols), lambda i, s: (s[i], 0)),
        )

        halfo = w_out.shape[0] // 2
        wo_half = lax.dynamic_slice_in_dim(w_out, parity * halfo, halfo, 0)
        wo_msg = jnp.concatenate([wo_half, oa.T], 0)
        wo_all = jnp.stack([wo_msg] + [zx(wo_msg, j) for j in (1, 2, 3)])
        oa_t = jnp.concatenate([wo_all[j, halfo:] for j in range(4)], 1)
        wo_z = wo_all[:, :halfo]
        out_cols = w_out.shape[1]
        wo_parts = [wo_z] + [wx(wo_z, j) for j in (1, 2, 3)]
        wo_parts = [part[:, None] for part in wo_parts + [cx(part, 1) for part in wo_parts]]
        wo = fold(
            jnp.concatenate([spots + 4 * parity, spots + 4 * (1 - parity)]),
            wo_parts,
            oa_t.T.reshape(4, 2, halfo, rank),
            ob,
            (4, 2, halfo, width),
            (4, 1, halfo, out_cols),
            pl.BlockSpec((4, 1, halfo, rank), lambda i, s: (0, s[i] // 4, 0, 0)),
            pl.BlockSpec((rank, out_cols), lambda i, s: (0, s[i] % 4)),
            pl.BlockSpec((4, 1, halfo, out_cols), lambda i, s: (0, s[i] // 4, 0, s[i] % 4)),
        ).reshape(width, width)

        up_rows = w_up.shape[0]
        units = w_up.shape[1]
        up_msg = jnp.concatenate(
            [w_up, ub, da.T, jnp.broadcast_to(up_bias[None], (rank, units))], 0
        )
        up_msg = cross(up_msg)
        wu_own = up_msg[:up_rows]
        ub = up_msg[up_rows : up_rows + rank]
        da_t = up_msg[up_rows + rank : up_rows + 2 * rank]
        bias_up = up_msg[up_rows + 2 * rank].astype(F32)
        wd_own = cross(w_down)
        wu = fold(
            spots,
            [wu_own] + [wx(wu_own, j) for j in (1, 2, 3)],
            ua,
            ub,
            (width, units),
            (up_rows, units),
            pl.BlockSpec((up_rows, rank), lambda i, s: (s[i], 0)),
            pl.BlockSpec((rank, units), lambda i, s: (0, 0)),
            pl.BlockSpec((up_rows, units), lambda i, s: (s[i], 0)),
        )
        wd = fold(
            spots,
            [wd_own] + [wx(wd_own, j) for j in (1, 2, 3)],
            da_t.T,
            db,
            (units, width),
            (units, out_cols),
            pl.BlockSpec((units, rank), lambda i, s: (0, 0)),
            pl.BlockSpec((rank, out_cols), lambda i, s: (0, s[i])),
            pl.BlockSpec((units, out_cols), lambda i, s: (0, s[i])),
        )

        def group_gather(value):
            pair = jnp.concatenate([value, zx(value, 1)], 0)
            return jnp.concatenate([pair, cx(pair, 1)], 0)

        def group_scatter(part):
            mine = part[: 2 * rows] + cx(part[2 * rows :].astype(BF), 1).astype(F32)
            return mine[:rows] + zx(mine[rows:].astype(BF), 1).astype(F32)

        dout = cotangent[0]
        doutg = group_gather(dout)

        bias_rows = jnp.concatenate(
            [qv_bias[0].astype(F32), jnp.zeros((cols,), F32), qv_bias[1].astype(F32)]
        )
        qkv = (mm(h1s, wq) + bias_rows).astype(BF)
        uq = mm(h1s, qa).astype(BF)
        q = qkv[:, :cols]
        kv = qkv[:, cols:]
        id_blocks = block_ids[0].reshape(n_context, n_tensor, rows)
        order = [zi ^ j for j in range(4)]
        id_rel = jnp.stack(
            [lax.dynamic_index_in_dim(id_blocks, spot, 1, keepdims=False) for spot in order], 1
        ).reshape(n_context, stretch)
        query_ids = lax.dynamic_index_in_dim(id_rel, ci, 0, keepdims=False)
        if n_context == 2:
            kv_all = jnp.concatenate([kv, cx(kv, 1)], 0)
            key_ids = jnp.concatenate(
                [query_ids, lax.dynamic_index_in_dim(id_rel, 1 - ci, 0, keepdims=False)]
            )
        else:
            kv_all = lax.all_gather(kv, "context", axis=0, tiled=True)
            key_ids = id_rel.reshape(-1)
        total = kv_all.shape[0]
        span = min(1024, total)
        blocks = total // span
        score_scale = HEAD ** (-0.5)
        qh = q.reshape(stretch, heads, HEAD)

        def key_part(index):
            piece = lax.dynamic_slice_in_dim(kv_all, index * span, span, 0)
            keys = piece[:, :cols].reshape(span, heads, HEAD)
            values = piece[:, cols:].reshape(span, heads, HEAD)
            return keys, values, lax.dynamic_slice_in_dim(key_ids, index * span, span, 0)

        def looped(step, start):
            if blocks == 1:
                state, out = step(start, 0)
                return state, None if out is None else jax.tree.map(lambda v: v[None], out)
            return lax.scan(step, start, jnp.arange(blocks))

        def stat_step(running, index):
            peak, mass = running
            keys, _, ids = key_part(index)
            scores = masked_scores(qh, keys, ids, query_ids)
            new_peak = jnp.maximum(peak, jnp.max(scores, axis=-1))
            mass = mass * jnp.exp(peak - new_peak) + jnp.sum(
                jnp.exp(scores - new_peak[..., None]), axis=-1
            )
            return (new_peak, mass), None

        (peak, mass), _ = looped(
            stat_step,
            (jnp.full((heads, stretch), -1e30, F32), jnp.zeros((heads, stretch), F32)),
        )
        lse = peak + jnp.log(mass)

        def value_step(running, index):
            keys, values, ids = key_part(index)
            scores = masked_scores(qh, keys, ids, query_ids)
            probs = jnp.exp(scores - lse[..., None]).astype(BF)
            return (
                running + jnp.einsum("hqk,khe->qhe", probs, values, preferred_element_type=F32),
                None,
            )

        attended, _ = looped(value_step, jnp.zeros((stretch, heads, HEAD), F32))
        att = attended.reshape(stretch, cols).astype(BF)
        att_blocks = [att[j * rows : (j + 1) * rows] for j in range(4)]
        attn = jnp.concatenate(
            [att_blocks[0]] + [zx(att_blocks[j], j) for j in (1, 2, 3)], 1
        )

        uo = mm_nt(attn, oa_t).astype(BF)
        middle = x + mm(attn, wo) + out_bias.astype(F32)
        unit2, scale2 = norm_stats(middle)
        h2 = (unit2 * gain2 + ln2_bias.astype(F32)).astype(BF)

        h2g = group_gather(h2)
        uu = mm(h2g, ua).astype(BF)
        up = mm(h2g, wu) + bias_up
        activated, gelu_back = jax.vjp(gelu_tanh, up)
        act = activated.astype(BF)
        dact = mm_nt(doutg, wd)
        dup = gelu_back(dact)[0].astype(BF)
        dh2 = group_scatter(mm_nt(dup, wu))
        mlp = group_scatter(mm(act, wd))
        block_out = middle + mlp + down_bias.astype(F32)
        dud = mm_nt(doutg, db).astype(BF)
        ud = mm_nt(act, da_t).astype(BF)
        duu = mm_nt(dup, ub).astype(BF)
        ua_g = mm_tn(duu, h2g)
        db_g = mm_tn(ud, doutg)
        ub_g = mm_tn(uu, dup)
        da_g = mm_tn(dud, act)

        first = jnp.concatenate([ua_g, db_g, ub_g, da_g], 0)
        first = first + zx(first.astype(BF), 2).astype(F32)
        shared = first[: 2 * rank] + zx(first[: 2 * rank].astype(BF), 1).astype(F32)
        split = first[2 * rank :]
        if n_context == 2:
            mine = jnp.concatenate([shared, split], 0)
            other = cx(mine.astype(BF), 1).astype(F32)
            shared = mine[: 2 * rank] + other[: 2 * rank]
            split = jnp.where(home, mine[2 * rank :], other[2 * rank :])
        else:
            shared = lax.psum(shared, "context")
            split = lax.psum(jnp.where(home, split, 0.0), "context")
        tag = jnp.full((rank, units), adapter, jnp.int32).astype(F32)
        packed = jnp.concatenate([shared, split, tag], 0).astype(BF)

        def weight_gather(value):
            pair = jnp.stack([value, wx(value, 1)])
            return jnp.concatenate([pair, wx(pair, 2)], 0)

        got1 = weight_gather(packed).astype(F32)
        owners = got1[:, -1, 0]
        slots = jnp.arange(qkv_a.shape[0]).astype(F32)
        choose = (slots[:, None] == owners[None, :])[:, :, None, None]

        def placed(values):
            return jnp.sum(jnp.where(choose, values[None], 0.0), axis=1)

        dmid = dout.astype(F32) + norm_back(unit2, scale2, dh2 * gain2)
        gz = dmid.astype(BF)
        duo = mm_nt(gz, ob).astype(BF)
        ob_g = mm_tn(uo, gz)
        oa_part = mm_tn(duo, attn)
        dattn = mm_nt(gz, wo).astype(BF)
        dat = jnp.concatenate(
            [dattn[:, :cols]]
            + [zx(dattn[:, j * cols : (j + 1) * cols], j) for j in (1, 2, 3)],
            0,
        )
        dh = dat.reshape(stretch, heads, HEAD)
        row_dot = jnp.einsum("qhe,qhe->hq", dh.astype(F32), attended)

        def back_step(grad_query, index):
            keys, values, ids = key_part(index)
            scores = masked_scores(qh, keys, ids, query_ids)
            probs = jnp.exp(scores - lse[..., None])
            grad_prob = jnp.einsum("qhe,khe->hqk", dh, values, preferred_element_type=F32)
            grad_score = (probs * (grad_prob - row_dot[..., None])).astype(BF)
            grad_query = grad_query + jnp.einsum(
                "hqk,khe->qhe", grad_score, keys, preferred_element_type=F32
            )
            grad_key = jnp.einsum("hqk,qhe->khe", grad_score, qh, preferred_element_type=F32)
            grad_value = jnp.einsum(
                "hqk,qhe->khe", probs.astype(BF), dh, preferred_element_type=F32
            )
            grad_kv = jnp.concatenate(
                [
                    grad_key.reshape(span, cols) * score_scale,
                    grad_value.reshape(span, cols),
                ],
                1,
            )
            return grad_query, grad_kv

        grad_query, grad_kv = looped(back_step, jnp.zeros((stretch, heads, HEAD), F32))
        grad_kv = grad_kv.reshape(total, 2 * cols)
        if n_context == 2:
            grad_kv = grad_kv[:stretch] + cx(grad_kv[stretch:].astype(BF), 1).astype(F32)
        else:
            grad_kv = lax.psum_scatter(
                grad_kv.astype(BF), "context", scatter_dimension=0, tiled=True
            ).astype(F32)
        dqkv = jnp.concatenate(
            [(grad_query * score_scale).reshape(stretch, cols), grad_kv], 1
        ).astype(BF)

        dh1_part = mm_nt(dqkv, wq)
        pieces = [dh1_part[j * rows : (j + 1) * rows] for j in range(4)]
        through = pieces[2] + zx(pieces[3].astype(BF), 1).astype(F32)
        dh1 = (
            pieces[0]
            + zx(pieces[1].astype(BF), 1).astype(F32)
            + zx(through.astype(BF), 2).astype(F32)
        )
        x_grad = dmid + norm_back(unit1, scale1, dh1 * gain1)

        duq = mm_nt(dqkv, qb).astype(BF)
        qa_g = mm_tn(duq, h1s)
        qb_g = mm_tn(uq, dqkv)
        last = jnp.concatenate([ob_g, qa_g], 0)
        side = [oa_part[:, j * cols : (j + 1) * cols] for j in range(4)]
        hop = jnp.concatenate(
            [last, jnp.concatenate([side[1], side[3], side[1], side[3]], 1)], 0
        )
        hop = zx(hop.astype(BF), 1).astype(F32)
        last = last + hop[: 2 * rank]
        own = side[0] + hop[2 * rank :, :cols]
        via = side[2] + hop[2 * rank :, cols : 2 * cols]
        hop = jnp.concatenate([last, jnp.concatenate([via, via, via, via], 1)], 0)
        hop = zx(hop.astype(BF), 2).astype(F32)
        last = last + hop[: 2 * rank]
        own = own + hop[2 * rank :, :cols]
        last = jnp.concatenate([last, jnp.concatenate([qb_g, own], 1)], 0)
        last = context_sum(last)
        got2 = weight_gather(last.astype(BF)).astype(F32)

        qkv_a_grad = placed(got2[:, rank : 2 * rank]).transpose(0, 2, 1)
        qkv_b_grad = placed(got2[:, 2 * rank :, : 3 * cols]).reshape(-1, rank, 3, cols)
        out_a_grad = placed(got2[:, 2 * rank :, 3 * cols :]).transpose(0, 2, 1)
        out_b_grad = placed(got2[:, :rank])
        up_a_grad = placed(got1[:, :rank]).transpose(0, 2, 1)
        up_b_grad = placed(got1[:, 2 * rank : 3 * rank])
        down_a_grad = placed(got1[:, 3 * rank : 4 * rank]).transpose(0, 2, 1)
        down_b_grad = placed(got1[:, rank : 2 * rank])
        return (
            block_out.astype(BF)[None],
            x_grad.astype(BF)[None],
            qkv_a_grad,
            qkv_b_grad,
            out_a_grad,
            out_b_grad,
            up_a_grad,
            up_b_grad,
            down_a_grad,
            down_b_grad,
        )

    return on_device


def solution(mesh):
    return jax.shard_map(
        make_device(mesh.shape["weight"], mesh.shape["context"], mesh.shape["tensor"]),
        mesh=mesh,
        in_specs=(
            P("weight", ("context", "tensor"), None),
            P("weight", None),
            P("weight"),
            P(),
            P(),
            P("weight", None, "tensor"),
            P(None, "tensor"),
            P("tensor", "weight"),
            P(),
            P(),
            P(),
            P("weight", "tensor"),
            P("tensor"),
            P("tensor", "weight"),
            P(),
            P(),
            P(None, None, None, "tensor"),
            P(None, "tensor", None),
            P(),
            P(),
            P(None, None, "tensor"),
            P(None, "tensor", None),
            P(),
            P("weight", ("context", "tensor"), None),
        ),
        out_specs=(
            P("weight", ("context", "tensor"), None),
            P("weight", ("context", "tensor"), None),
            P(),
            P(None, None, None, "tensor"),
            P(None, "tensor", None),
            P(),
            P(),
            P(None, None, "tensor"),
            P(None, "tensor", None),
            P(),
        ),
        check_vma=False,
    )
```
